768 devices in a mesh: rep: 16 (over x_hi, y), row: 4 (over x_lo, core), col: 12 (over z).
Axes of the slice: x: 4 (x_hi: 2, x_lo: 2; x = x_hi * 2 + x_lo), y: 8, z: 12, core: 2. Of those that a mesh axis runs over, the one named last changes fastest.
Arguments:
- normed: bfloat16 [8192, 5120], P('rep', 'row'), may hold values from -6 to 6
- up_weight: bfloat16 [4, 1280, 13824], P('row', 'rep', 'col'), may hold values from -0.078125 to 0.078125
- cotangent: bfloat16 [8192, 13824], P('rep', 'col'), may hold values from -6 to 6
- lengths: int32 [16], P('rep'), may hold values from 128 to 512
Outputs:
- up_out: bfloat16 [8192, 13824], P(('rep', 'row'), 'col')
- normed_grad: bfloat16 [8192, 5120], P('rep', 'row')
- weight_grad: bfloat16 [4, 1280, 13824], P('row', 'rep', 'col')
The draws below stay inside these ranges and needn't reach their ends.
All inputs are finite; a program needn't handle non-finite values.
Results may differ from the reference program's by a relative error of at most 0.02.
Values may be sent and summed in bfloat16 or wider, within the bound.
No kernel may reach another device: no remote copies, remote signals or barrier semaphores. Data moves between devices by JAX's collectives and lax.ppermute only.
A program may use at most 32 MiB of HBM per device.

```python
import math
import jax
import jax.numpy as jnp
from jax import lax

D = 5120
FF = 13824
LEN = 512
TOK_REP = 512
PAIRS = 16
TOKENS = 8192
N_REP = 16
N_ROW = 4
N_COL = 12


def with_ends(result, rng, low, top_value):
    longest = result.shape.index(max(result.shape))
    spots = []
    for shift in (0, 1):
        where = [jax.random.randint(jax.random.fold_in(rng, axis), (), 0, length) for axis, length in enumerate(result.shape)]
        where[longest] = (where[longest] + shift) % result.shape[longest]
        spots.append(tuple(where))
    return result.at[spots[0]].set(low).at[spots[1]].set(top_value)


def shard_levels(stream_key, dims, pieces, smallest, largest):
    loudness = 1.0
    for axis_at, shards_of in pieces:
        draws = jax.random.uniform(jax.random.fold_in(jax.random.fold_in(stream_key, 6), axis_at), (shards_of,), jnp.float32, smallest / len(pieces), largest / len(pieces))
        loudness = loudness * jnp.repeat(jnp.exp(draws), dims[axis_at] // shards_of).reshape((-1,) + (1,) * (len(dims) - 1 - axis_at))
    return loudness


def noise(own_key, dims, width, reach, pieces=(), kind=jnp.bfloat16):
    result = width * jax.random.normal(own_key, dims, jnp.float32)
    if pieces:
        result = result * shard_levels(own_key, dims, pieces, -0.22, 0.18)
    return jnp.clip(result, -reach, reach).astype(kind)


def setup_inputs(seed: int = 0) -> dict:
    keys = jax.random.split(jax.random.key(seed), 5)
    return {
        "normed": noise(keys[0], (TOKENS, D), 1.0, 6.0, ((0, 16), (1, 4))),
        "up_weight": noise(keys[1], (N_ROW, D // N_ROW, FF), D ** -0.5, 0.078125, ((0, 4), (1, 16), (2, 12))),
        "cotangent": noise(keys[2], (TOKENS, FF), 1.0, 6.0, ((0, 16), (1, 12))),
        "lengths": with_ends(jax.random.randint(keys[3], (PAIRS,), LEN // 4, LEN + 1), jax.random.fold_in(keys[3], 1), LEN // 4, LEN).astype(jnp.int32),
    }


def rounded(value):
    return lax.optimization_barrier(value.astype(jnp.bfloat16)).astype(jnp.float32)

def reference(normed, up_weight, cotangent, lengths):
    weight = up_weight.reshape(D, FF)
    block_width = D // N_ROW
    up_total = jnp.zeros((TOKENS, FF), jnp.float32)
    for block_index in range(N_ROW):
        low = block_index * block_width
        partial_value = jnp.dot(normed[:, low:low + block_width], weight[low:low + block_width], preferred_element_type=jnp.float32)
        up_total = up_total + rounded(partial_value)
    positions = jnp.arange(LEN, dtype=jnp.int32)
    valid_rows = (positions[None, :] < lengths[:, None]).reshape(TOKENS, 1)
    masked = jnp.where(valid_rows, cotangent, jnp.zeros_like(cotangent))
    unit_width = FF // N_COL
    grad_total = jnp.zeros((TOKENS, D), jnp.float32)
    for block_index in range(N_COL):
        low = block_index * unit_width
        partial_value = lax.dot_general(masked[:, low:low + unit_width], weight[:, low:low + unit_width], (((1,), (1,)), ((), ())), preferred_element_type=jnp.float32)
        grad_total = grad_total + rounded(partial_value)
    factor = 1.0 / math.sqrt(TOKENS)
    weight_total = jnp.zeros((D, FF), jnp.float32)
    for block_index in range(N_REP):
        low = block_index * TOK_REP
        partial_value = lax.dot_general(normed[low:low + TOK_REP], masked[low:low + TOK_REP], (((0,), (0,)), ((), ())), preferred_element_type=jnp.float32)
        weight_total = weight_total + rounded(partial_value * factor)
    return (up_total.astype(jnp.bfloat16), grad_total.astype(jnp.bfloat16), weight_total.astype(jnp.bfloat16).reshape(N_ROW, D // N_ROW, FF))
```

```python
import math

import jax
import jax.numpy as jnp
from jax import lax
from jax.sharding import PartitionSpec as P

NY = 8
NZ = 12
F32 = jnp.float32
BF16 = jnp.bfloat16

X_SWAP = [(i, (i + NY) % (2 * NY)) for i in range(2 * NY)]


def y_shift(step):
    return [(h * NY + y, h * NY + (y + step) % NY) for h in range(2) for y in range(NY)]


def z_shift(step):
    return [(z, (z + step) % NZ) for z in range(NZ)]


def over_rep(value, pairs):
    return lax.ppermute(value, "rep", pairs)


def over_col(value, step):
    return lax.ppermute(value, "col", z_shift(step))


def add(*terms):
    total = terms[0].astype(F32)
    for term in terms[1:]:
        total = total + term.astype(F32)
    return total.astype(BF16)


def pick(blocks, index):
    return lax.dynamic_index_in_dim(blocks, index, 0, keepdims=True)


def gather_weight(w0, x_hi, y):
    from_m3 = over_rep(w0, y_shift(3))
    from_p3 = over_rep(w0, y_shift(-3))
    three = jnp.concatenate([w0, from_p3, from_m3])
    from_m1 = over_rep(three, y_shift(1))
    from_p1 = over_rep(jnp.concatenate([w0, from_m3]), y_shift(-1))
    other_three = over_rep(three, X_SWAP)
    five = jnp.concatenate([from_m1, from_p1])
    other_five = over_rep(five, X_SWAP)
    whole = jnp.zeros((16,) + w0.shape[1:], w0.dtype)
    for half, low, high in ((x_hi, three, five), (1 - x_hi, other_three, other_five)):
        for source, steps in ((low, (0, 3, -3)), (high, (-1, 2, 4, 1, -2))):
            for slot, step in enumerate(steps):
                place = half * NY + lax.rem(y + step + NY, NY)
                whole = lax.dynamic_update_slice(
                    whole, source[slot : slot + 1], (place, 0, 0)
                )
    return whole.reshape(-1, w0.shape[2])


def scatter_wgrad(normed, masked, factor, x_hi, y, keep_rows):
    half = normed.shape[1] // 2
    left, right = normed[:, :half], normed[:, half:]
    first = x_hi == 0

    def product(columns):
        value = lax.dot_general(
            columns, masked, (((0,), (0,)), ((), ())), preferred_element_type=F32
        )
        return (value * factor).astype(BF16).reshape(NY, keep_rows, -1)

    sent = product(jnp.where(first, right, left))
    came = over_rep(sent, X_SWAP)
    mine = product(jnp.where(first, left, right))
    both = add(mine, came)

    def block(step):
        return pick(both, lax.rem(y + step + NY, NY))

    up1 = over_rep(jnp.concatenate([block(1), block(4), block(-2)]), y_shift(1))
    down1 = over_rep(jnp.concatenate([block(-1), block(2)]), y_shift(-1))
    plus3 = over_rep(add(block(3), up1[1:2], down1[1:2]), y_shift(3))
    minus3 = over_rep(add(block(-3), up1[2:3]), y_shift(-3))
    return add(block(0), up1[0:1], down1[0:1], plus3, minus3)


def body(normed, up_weight, cotangent, lengths):
    row_count, width = normed.shape
    pair_count = lengths.shape[0]
    pair_len = row_count // pair_count
    keep_rows, unit_count = up_weight.shape[1:]
    rep = lax.axis_index("rep")
    x_hi, y = rep // NY, lax.rem(rep, NY)
    row = lax.axis_index("row")
    z = lax.axis_index("col")

    weight = gather_weight(up_weight, x_hi, y)

    positions = lax.broadcasted_iota(jnp.int32, (pair_count, pair_len), 1)
    valid_rows = (positions < lengths[:, None]).reshape(row_count, 1)
    masked = jnp.where(valid_rows, cotangent, jnp.zeros_like(cotangent))

    factor = 1.0 / math.sqrt(row_count * lax.axis_size("rep"))
    weight_grad = scatter_wgrad(normed, masked, factor, x_hi, y, keep_rows)

    unit_rows = -(-row_count // (NZ * 16)) * 16
    padded = jnp.pad(masked, ((0, NZ * unit_rows - row_count), (0, 0)))
    grid = padded.reshape(NZ // 3, 3, unit_rows, unit_count)

    def partial_grad(step):
        tokens = lax.dynamic_index_in_dim(grid, lax.rem(z + step + NZ, 3), 1, keepdims=False)
        value = lax.dot_general(
            tokens.reshape(-1, unit_count),
            weight,
            (((1,), (1,)), ((), ())),
            preferred_element_type=F32,
        )
        return value.astype(BF16).reshape(NZ // 3, unit_rows, width)

    up1 = over_col(partial_grad(1), 1)
    down1 = over_col(partial_grad(-1), -1)
    four = add(partial_grad(0), up1, down1)
    q = z // 3

    def unit(step):
        return pick(four, lax.rem(q + step + 4, 4))

    plus3 = over_col(unit(1), 3)
    minus3 = over_col(unit(-1), -3)
    plus6 = over_col(unit(2), 6)
    own = add(unit(0), plus3, minus3, plus6)
    got = jnp.zeros((NZ // 3, unit_rows, width), BF16)
    for step, value in (
        (0, own),
        (-1, over_col(own, 3)),
        (1, over_col(own, -3)),
        (2, over_col(own, 6)),
    ):
        got = lax.dynamic_update_slice(got, value, (lax.rem(q + step + 4, 4), 0, 0))
    result = jnp.zeros((NZ // 3, 3, unit_rows, width), BF16)
    for step, value in ((0, got), (-1, over_col(got, 1)), (1, over_col(got, -1))):
        result = lax.dynamic_update_slice(
            result, value[:, None], (0, lax.rem(z + step + NZ, 3), 0, 0)
        )
    normed_grad = result.reshape(NZ * unit_rows, width)[:row_count]

    parts = normed.reshape(4, row_count // 4, width)
    parts = jnp.where(row // 2 == 0, parts, jnp.concatenate([parts[2:], parts[:2]]))
    even = jnp.concatenate([parts[0:1], parts[2:3]])
    odd = jnp.concatenate([parts[1:2], parts[3:4]])
    core = lax.rem(row, 2)

    def partial_up(tokens):
        value = jnp.dot(tokens.reshape(-1, width), weight, preferred_element_type=F32)
        return value.astype(BF16).reshape(2, row_count // 4, unit_count)

    came = lax.ppermute(
        partial_up(jnp.where(core == 0, odd, even)), "row", [(r, r ^ 1) for r in range(4)]
    )
    two = add(partial_up(jnp.where(core == 0, even, odd)), came)
    came = lax.ppermute(two[1], "row", [(r, r ^ 2) for r in range(4)])
    up_out = add(two[0], came)
    return (up_out, normed_grad, weight_grad)


def solution(mesh):
    placed = (P("rep", "row"), P("row", "rep", "col"), P("rep", "col"), P("rep"))
    return jax.shard_map(
        body,
        mesh=mesh,
        in_specs=placed,
        out_specs=(P(("rep", "row"), "col"), P("rep", "row"), P("row", "rep", "col")),
        check_vma=False,
    )
```

```python
import math

import jax
import jax.numpy as jnp
from jax import lax
from jax.sharding import PartitionSpec as P

NY = 8
NZ = 12
F32 = jnp.float32
BF16 = jnp.bfloat16

X_PAIRS = [[y, y + NY] for y in range(NY)]
Y_RINGS = [[h * NY + y for y in range(NY)] for h in range(2)]
X_SWAP = [(i, (i + NY) % (2 * NY)) for i in range(2 * NY)]


def z_shift(step):
    return [(z, (z + step) % NZ) for z in range(NZ)]


def over_rep(value, pairs):
    return lax.ppermute(value, "rep", pairs)


def over_col(value, step):
    return lax.ppermute(value, "col", z_shift(step))


def add(*terms):
    total = terms[0].astype(F32)
    for term in terms[1:]:
        total = total + term.astype(F32)
    return total.astype(BF16)


def pick(blocks, index):
    return lax.dynamic_index_in_dim(blocks, index, 0, keepdims=True)


def gather_weight(w0):
    pair = lax.all_gather(w0, "rep", axis=0, tiled=True, axis_index_groups=X_PAIRS)
    whole = lax.all_gather(pair, "rep", axis=1, tiled=True, axis_index_groups=Y_RINGS)
    return whole.reshape(-1, w0.shape[2])


def scatter_wgrad(normed, masked, factor, x_hi, keep_rows):
    value = lax.dot_general(
        normed, masked, (((0,), (0,)), ((), ())), preferred_element_type=F32
    )
    value = (value * factor).astype(BF16).reshape(2, NY, keep_rows, -1)
    value = value.transpose(1, 0, 2, 3).reshape(NY * 2, keep_rows, -1)
    pair = lax.psum_scatter(
        value, "rep", scatter_dimension=0, tiled=True, axis_index_groups=Y_RINGS
    )
    came = over_rep(pick(pair, 1 - x_hi), X_SWAP)
    return add(pick(pair, x_hi), came)


def body(normed, up_weight, cotangent, lengths):
    row_count, width = normed.shape
    pair_count = lengths.shape[0]
    pair_len = row_count // pair_count
    keep_rows, unit_count = up_weight.shape[1:]
    rep = lax.axis_index("rep")
    x_hi = rep // NY
    row = lax.axis_index("row")
    z = lax.axis_index("col")

    weight = gather_weight(up_weight)

    positions = lax.broadcasted_iota(jnp.int32, (pair_count, pair_len), 1)
    valid_rows = (positions < lengths[:, None]).reshape(row_count, 1)
    masked = jnp.where(valid_rows, cotangent, jnp.zeros_like(cotangent))

    factor = 1.0 / math.sqrt(row_count * lax.axis_size("rep"))
    weight_grad = scatter_wgrad(normed, masked, factor, x_hi, keep_rows)

    unit_rows = -(-row_count // (NZ * 16)) * 16
    padded = jnp.pad(masked, ((0, NZ * unit_rows - row_count), (0, 0)))
    grid = padded.reshape(NZ // 3, 3, unit_rows, unit_count)

    def partial_grad(step):
        tokens = lax.dynamic_index_in_dim(grid, lax.rem(z + step + NZ, 3), 1, keepdims=False)
        value = lax.dot_general(
            tokens.reshape(-1, unit_count),
            weight,
            (((1,), (1,)), ((), ())),
            preferred_element_type=F32,
        )
        return value.astype(BF16).reshape(NZ // 3, unit_rows, width)

    up1 = over_col(partial_grad(1), 1)
    down1 = over_col(partial_grad(-1), -1)
    four = add(partial_grad(0), up1, down1)
    q = z // 3

    def unit(step):
        return pick(four, lax.rem(q + step + 4, 4))

    plus3 = over_col(unit(1), 3)
    minus3 = over_col(unit(-1), -3)
    plus6 = over_col(unit(2), 6)
    own = add(unit(0), plus3, minus3, plus6)
    got = jnp.zeros((NZ // 3, unit_rows, width), BF16)
    for step, value in (
        (0, own),
        (-1, over_col(own, 3)),
        (1, over_col(own, -3)),
        (2, over_col(own, 6)),
    ):
        got = lax.dynamic_update_slice(got, value, (lax.rem(q + step + 4, 4), 0, 0))
    result = jnp.zeros((NZ // 3, 3, unit_rows, width), BF16)
    for step, value in ((0, got), (-1, over_col(got, 1)), (1, over_col(got, -1))):
        result = lax.dynamic_update_slice(
            result, value[:, None], (0, lax.rem(z + step + NZ, 3), 0, 0)
        )
    normed_grad = result.reshape(NZ * unit_rows, width)[:row_count]

    parts = normed.reshape(4, row_count // 4, width)
    parts = jnp.where(row // 2 == 0, parts, jnp.concatenate([parts[2:], parts[:2]]))
    even = jnp.concatenate([parts[0:1], parts[2:3]])
    odd = jnp.concatenate([parts[1:2], parts[3:4]])
    core = lax.rem(row, 2)

    def partial_up(tokens):
        value = jnp.dot(tokens.reshape(-1, width), weight, preferred_element_type=F32)
        return value.astype(BF16).reshape(2, row_count // 4, unit_count)

    came = lax.ppermute(
        partial_up(jnp.where(core == 0, odd, even)), "row", [(r, r ^ 1) for r in range(4)]
    )
    two = add(partial_up(jnp.where(core == 0, even, odd)), came)
    came = lax.ppermute(two[1], "row", [(r, r ^ 2) for r in range(4)])
    up_out = add(two[0], came)
    return (up_out, normed_grad, weight_grad)


def solution(mesh):
    placed = (P("rep", "row"), P("row", "rep", "col"), P("rep", "col"), P("rep"))
    return jax.shard_map(
        body,
        mesh=mesh,
        in_specs=placed,
        out_specs=(P(("rep", "row"), "col"), P("rep", "row"), P("row", "rep", "col")),
        check_vma=False,
    )
```

```python
import math

import jax
import jax.numpy as jnp
from jax import lax
from jax.sharding import PartitionSpec as P

NY = 8
NZ = 12
F32 = jnp.float32
BF16 = jnp.bfloat16

Y_RINGS = [[h * NY + y for y in range(NY)] for h in range(2)]
X_SWAP = [(i, (i + NY) % (2 * NY)) for i in range(2 * NY)]


def y_shift(step):
    return [(h * NY + y, h * NY + (y + step) % NY) for h in range(2) for y in range(NY)]


def z_shift(step):
    return [(z, (z + step) % NZ) for z in range(NZ)]


def over_rep(value, pairs):
    return lax.ppermute(value, "rep", pairs)


def over_col(value, step):
    return lax.ppermute(value, "col", z_shift(step))


def add(*terms):
    total = terms[0].astype(F32)
    for term in terms[1:]:
        total = total + term.astype(F32)
    return total.astype(BF16)


def pick(blocks, index):
    return lax.dynamic_index_in_dim(blocks, index, 0, keepdims=True)


def gather_weight(w0, y):
    own = lax.all_gather(w0, "rep", axis=1, tiled=True, axis_index_groups=Y_RINGS)
    there = over_rep(w0, X_SWAP)
    from_m3 = over_rep(there, y_shift(3))
    from_p3 = over_rep(there, y_shift(-3))
    from_m1 = over_rep(jnp.concatenate([there, from_p3, from_m3]), y_shift(1))
    from_p1 = over_rep(jnp.concatenate([there, from_m3]), y_shift(-1))
    other = jnp.zeros((NY,) + w0.shape[1:], w0.dtype)
    for source, steps in (
        (there, (0,)),
        (from_m3, (-3,)),
        (from_p3, (3,)),
        (from_m1, (-1, 2, 4)),
        (from_p1, (1, -2)),
    ):
        for slot, step in enumerate(steps):
            place = lax.rem(y + step + NY, NY)
            other = lax.dynamic_update_slice(
                other, source[slot : slot + 1], (place, 0, 0)
            )
    return jnp.concatenate([own[0], other.reshape(own.shape[1:])])


def scatter_wgrad(halves, masked, factor):
    def product(columns):
        value = lax.dot_general(
            columns, masked, (((0,), (0,)), ((), ())), preferred_element_type=F32
        )
        return (value * factor).astype(BF16)

    came = over_rep(product(halves[1]), X_SWAP)
    both = add(product(halves[0]), came)
    return lax.psum_scatter(
        both, "rep", scatter_dimension=0, tiled=True, axis_index_groups=Y_RINGS
    )


def body(normed, up_weight, cotangent, lengths):
    row_count, width = normed.shape
    pair_count = lengths.shape[0]
    pair_len = row_count // pair_count
    keep_rows, unit_count = up_weight.shape[1:]
    rep = lax.axis_index("rep")
    y = lax.rem(rep, NY)
    first = rep < NY
    z = lax.axis_index("col")

    def swap_halves(columns):
        left, right = columns[:, : width // 2], columns[:, width // 2 :]
        return jnp.where(first, left, right), jnp.where(first, right, left)

    weight = gather_weight(up_weight, y)

    positions = lax.broadcasted_iota(jnp.int32, (pair_count, pair_len), 1)
    valid_rows = (positions < lengths[:, None]).reshape(row_count, 1)
    masked = jnp.where(valid_rows, cotangent, jnp.zeros_like(cotangent))

    factor = 1.0 / math.sqrt(row_count * lax.axis_size("rep"))
    halves = swap_halves(normed)
    weight_grad = scatter_wgrad(halves, masked, factor)
    weight_grad = weight_grad.reshape(1, keep_rows, unit_count)

    unit_rows = -(-row_count // (NZ * 16)) * 16
    padded = jnp.pad(masked, ((0, NZ * unit_rows - row_count), (0, 0)))
    grid = padded.reshape(NZ // 3, 3, unit_rows, unit_count)

    def partial_grad(step):
        tokens = lax.dynamic_index_in_dim(grid, lax.rem(z + step + NZ, 3), 1, keepdims=False)
        value = lax.dot_general(
            tokens.reshape(-1, unit_count),
            weight,
            (((1,), (1,)), ((), ())),
            preferred_element_type=F32,
        )
        return value.astype(BF16).reshape(NZ // 3, unit_rows, width)

    up1 = over_col(partial_grad(1), 1)
    down1 = over_col(partial_grad(-1), -1)
    four = add(partial_grad(0), up1, down1)
    q = z // 3

    def unit(step):
        return pick(four, lax.rem(q + step + 4, 4))

    plus3 = over_col(unit(1), 3)
    minus3 = over_col(unit(-1), -3)
    plus6 = over_col(unit(2), 6)
    own = add(unit(0), plus3, minus3, plus6)
    got = jnp.zeros((NZ // 3, unit_rows, width), BF16)
    for step, value in (
        (0, own),
        (-1, over_col(own, 3)),
        (1, over_col(own, -3)),
        (2, over_col(own, 6)),
    ):
        got = lax.dynamic_update_slice(got, value, (lax.rem(q + step + 4, 4), 0, 0))
    result = jnp.zeros((NZ // 3, 3, unit_rows, width), BF16)
    for step, value in ((0, got), (-1, over_col(got, 1)), (1, over_col(got, -1))):
        result = lax.dynamic_update_slice(
            result, value[:, None], (0, lax.rem(z + step + NZ, 3), 0, 0)
        )
    result = result.reshape(NZ * unit_rows, width)[:row_count]
    normed_grad = jnp.concatenate(swap_halves(result), axis=1)

    up_partial = jnp.dot(
        jnp.concatenate(halves, axis=1), weight, preferred_element_type=F32
    )
    up_out = lax.psum_scatter(
        up_partial.astype(BF16), "row", scatter_dimension=0, tiled=True
    )
    return (up_out, normed_grad, weight_grad)


def solution(mesh):
    placed = (P("rep", "row"), P("row", "rep", "col"), P("rep", "col"), P("rep"))
    return jax.shard_map(
        body,
        mesh=mesh,
        in_specs=placed,
        out_specs=(P(("rep", "row"), "col"), P("rep", "row"), P("row", "rep", "col")),
        check_vma=False,
    )
```

```python
import math

import jax
import jax.numpy as jnp
from jax import lax
from jax.sharding import PartitionSpec as P

NY = 8
NZ = 12
F32 = jnp.float32
BF16 = jnp.bfloat16

Y_RINGS = [[h * NY + y for y in range(NY)] for h in range(2)]
X_PAIRS = [[y, y + NY] for y in range(NY)]
X_SWAP = [(i, (i + NY) % (2 * NY)) for i in range(2 * NY)]


def z_shift(step):
    return [(z, (z + step) % NZ) for z in range(NZ)]


def over_rep(value, pairs):
    return lax.ppermute(value, "rep", pairs)


def over_col(value, step):
    return lax.ppermute(value, "col", z_shift(step))


def near_two(value):
    pairs = []
    for row in range(4):
        step = 2 - 4 * (row % 2)
        pairs += [(row * NZ + z, row * NZ + (z + step) % NZ) for z in range(NZ)]
    return lax.ppermute(value, ("row", "col"), pairs)


def add(*terms):
    total = terms[0].astype(F32)
    for term in terms[1:]:
        total = total + term.astype(F32)
    return total.astype(BF16)


def gather_weight(w0):
    pair = lax.all_gather(w0, "rep", axis=0, tiled=True, axis_index_groups=X_PAIRS)
    whole = lax.all_gather(pair, "rep", axis=1, tiled=True, axis_index_groups=Y_RINGS)
    return whole.reshape(-1, w0.shape[2])


def scatter_wgrad(normed, masked, factor, first):
    half = normed.shape[1] // 2
    left, right = normed[:, :half], normed[:, half:]

    def product(columns):
        value = lax.dot_general(
            columns, masked, (((0,), (0,)), ((), ())), preferred_element_type=F32
        )
        return (value * factor).astype(BF16)

    came = over_rep(product(jnp.where(first, right, left)), X_SWAP)
    both = add(product(jnp.where(first, left, right)), came)
    return lax.psum_scatter(
        both, "rep", scatter_dimension=0, tiled=True, axis_index_groups=Y_RINGS
    )


def sum_over_col(partial, z):
    def residue(step):
        return lax.rem(z + step + NZ, 4)

    def near(pieces):
        return (
            near_two(pieces[0]),
            over_col(pieces[1], 1),
            over_col(pieces[2], -1),
        )

    arrived = near((partial(residue(2)), partial(residue(1)), partial(residue(-1))))
    three = add(partial(residue(0)), *arrived)
    below = over_col(three, 4)
    above = over_col(three, -4)
    q = z // 4
    last = jnp.where(q == 0, below, jnp.where(q == 1, above, three))
    one = jnp.where(q == 0, three, below)
    two = jnp.where(q == 1, three, above)
    total = add(one, two, last)
    arrived = near((total, total, total))
    result = jnp.zeros((3, 4) + total.shape[1:], total.dtype)
    for step, value in ((0, total), (2, arrived[0]), (-1, arrived[1]), (1, arrived[2])):
        result = lax.dynamic_update_slice(result, value[:, None], (0, residue(step), 0, 0))
    return result.reshape(-1, total.shape[2])


def body(normed, up_weight, cotangent, lengths):
    row_count, width = normed.shape
    pair_count = lengths.shape[0]
    pair_len = row_count // pair_count
    keep_rows, unit_count = up_weight.shape[1:]
    first = lax.axis_index("rep") < NY
    z = lax.axis_index("col")

    weight = gather_weight(up_weight)

    positions = lax.broadcasted_iota(jnp.int32, (pair_count, pair_len), 1)
    valid_rows = (positions < lengths[:, None]).reshape(row_count, 1)
    masked = jnp.where(valid_rows, cotangent, jnp.zeros_like(cotangent))

    factor = 1.0 / math.sqrt(row_count * lax.axis_size("rep"))
    weight_grad = scatter_wgrad(normed, masked, factor, first)
    weight_grad = weight_grad.reshape(1, keep_rows, unit_count)

    unit_rows = -(-row_count // (NZ * 16)) * 16
    padded = jnp.pad(masked, ((0, NZ * unit_rows - row_count), (0, 0)))
    units = padded.reshape(3, 4, unit_rows, unit_count)

    def partial_grad(residue):
        tokens = lax.dynamic_index_in_dim(units, residue, 1, keepdims=False)
        value = lax.dot_general(
            tokens.reshape(-1, unit_count),
            weight,
            (((1,), (1,)), ((), ())),
            preferred_element_type=F32,
        )
        return value.astype(BF16).reshape(3, unit_rows, width)

    normed_grad = sum_over_col(partial_grad, z)[:row_count]

    up_partial = jnp.dot(normed, weight, preferred_element_type=F32)
    up_out = lax.psum_scatter(
        up_partial.astype(BF16), "row", scatter_dimension=0, tiled=True
    )
    return (up_out, normed_grad, weight_grad)


def solution(mesh):
    placed = (P("rep", "row"), P("row", "rep", "col"), P("rep", "col"), P("rep"))
    return jax.shard_map(
        body,
        mesh=mesh,
        in_specs=placed,
        out_specs=(P(("rep", "row"), "col"), P("rep", "row"), P("row", "rep", "col")),
        check_vma=False,
    )
```

```python
import math

import jax
import jax.numpy as jnp
from jax import lax
from jax.sharding import PartitionSpec as P

NY = 8
NZ = 12
F32 = jnp.float32
BF16 = jnp.bfloat16

Y_RINGS = [[h * NY + y for y in range(NY)] for h in range(2)]
X_PAIRS = [[y, y + NY] for y in range(NY)]
X_SWAP = [(i, (i + NY) % (2 * NY)) for i in range(2 * NY)]


def z_shift(step):
    return [(z, (z + step) % NZ) for z in range(NZ)]


def over_rep(value, pairs):
    return lax.ppermute(value, "rep", pairs)


def over_col(value, step):
    return lax.ppermute(value, "col", z_shift(step))


def near_two(value):
    pairs = []
    for row in range(4):
        step = 2 - 4 * (row % 2)
        pairs += [(row * NZ + z, row * NZ + (z + step) % NZ) for z in range(NZ)]
    return lax.ppermute(value, ("row", "col"), pairs)


def add(*terms):
    total = terms[0].astype(F32)
    for term in terms[1:]:
        total = total + term.astype(F32)
    return total.astype(BF16)


def gather_weight(w0):
    pair = lax.all_gather(w0, "rep", axis=0, tiled=True, axis_index_groups=X_PAIRS)
    whole = lax.all_gather(pair, "rep", axis=1, tiled=True, axis_index_groups=Y_RINGS)
    return whole.reshape(-1, w0.shape[2])


def scatter_wgrad(normed, masked, factor, first):
    half = normed.shape[1] // 2
    left, right = normed[:, :half], normed[:, half:]

    def product(columns):
        value = lax.dot_general(
            columns, masked, (((0,), (0,)), ((), ())), preferred_element_type=F32
        )
        return (value * factor).astype(BF16)

    came = over_rep(product(jnp.where(first, right, left)), X_SWAP)
    both = add(product(jnp.where(first, left, right)), came)
    return lax.psum_scatter(
        both, "rep", scatter_dimension=0, tiled=True, axis_index_groups=Y_RINGS
    )


def sum_over_col(partial, z):
    def residue(step):
        return lax.rem(z + step + NZ, 4)

    def near(pieces):
        return (
            near_two(pieces[0]),
            over_col(pieces[1], 1),
            over_col(pieces[2], -1),
        )

    arrived = near((partial(residue(2)), partial(residue(1)), partial(residue(-1))))
    mine = add(partial(residue(0)), *arrived)
    below = over_col(mine, 4)
    above = over_col(mine, -4)
    q = z // 4
    last = jnp.where(q == 0, below, jnp.where(q == 1, above, mine))
    one = jnp.where(q == 0, mine, below)
    two = jnp.where(q == 1, mine, above)
    total = add(one, two, last)
    arrived = near((total, total, total))
    result = jnp.zeros((4,) + total.shape, total.dtype)
    for step, value in ((0, total), (2, arrived[0]), (-1, arrived[1]), (1, arrived[2])):
        result = lax.dynamic_update_slice(result, value[None], (residue(step), 0, 0))
    return result.reshape(-1, total.shape[1])


def body(normed, up_weight, cotangent, lengths):
    row_count, width = normed.shape
    pair_count = lengths.shape[0]
    pair_len = row_count // pair_count
    keep_rows, unit_count = up_weight.shape[1:]
    first = lax.axis_index("rep") < NY
    z = lax.axis_index("col")

    weight = gather_weight(up_weight)

    positions = lax.broadcasted_iota(jnp.int32, (pair_count, pair_len), 1)
    valid_rows = (positions < lengths[:, None]).reshape(row_count, 1)
    masked = jnp.where(valid_rows, cotangent, jnp.zeros_like(cotangent))

    factor = 1.0 / math.sqrt(row_count * lax.axis_size("rep"))
    weight_grad = scatter_wgrad(normed, masked, factor, first)
    weight_grad = weight_grad.reshape(1, keep_rows, unit_count)

    quarters = masked.reshape(4, row_count // 4, unit_count)

    def partial_grad(quarter):
        tokens = lax.dynamic_index_in_dim(quarters, quarter, 0, keepdims=False)
        value = lax.dot_general(
            tokens, weight, (((1,), (1,)), ((), ())), preferred_element_type=F32
        )
        return value.astype(BF16)

    normed_grad = sum_over_col(partial_grad, z)

    up_partial = jnp.dot(normed, weight, preferred_element_type=F32)
    up_out = lax.psum_scatter(
        up_partial.astype(BF16), "row", scatter_dimension=0, tiled=True
    )
    return (up_out, normed_grad, weight_grad)


def solution(mesh):
    placed = (P("rep", "row"), P("row", "rep", "col"), P("rep", "col"), P("rep"))
    return jax.shard_map(
        body,
        mesh=mesh,
        in_specs=placed,
        out_specs=(P(("rep", "row"), "col"), P("rep", "row"), P("row", "rep", "col")),
        check_vma=False,
    )
```

```python
import math

import jax
import jax.numpy as jnp
from jax import lax
from jax.sharding import PartitionSpec as P

NY = 8
NZ = 12
F32 = jnp.float32
BF16 = jnp.bfloat16

Y_RINGS = [[h * NY + y for y in range(NY)] for h in range(2)]
X_PAIRS = [[y, y + NY] for y in range(NY)]
X_SWAP = [(i, (i + NY) % (2 * NY)) for i in range(2 * NY)]


def z_shift(step):
    return [(z, (z + step) % NZ) for z in range(NZ)]


def over_rep(value, pairs):
    return lax.ppermute(value, "rep", pairs)


def over_col(value, step):
    return lax.ppermute(value, "col", z_shift(step))


def near_two(value):
    pairs = []
    for row in range(4):
        step = 2 - 4 * (row % 2)
        pairs += [(row * NZ + z, row * NZ + (z + step) % NZ) for z in range(NZ)]
    return lax.ppermute(value, ("row", "col"), pairs)


def add(*terms):
    total = terms[0].astype(F32)
    for term in terms[1:]:
        total = total + term.astype(F32)
    return total.astype(BF16)


def gather_weight(w0):
    pair = lax.all_gather(w0, "rep", axis=0, tiled=True, axis_index_groups=X_PAIRS)
    whole = lax.all_gather(pair, "rep", axis=1, tiled=True, axis_index_groups=Y_RINGS)
    return whole.reshape(-1, w0.shape[2])


def scatter_wgrad(normed, masked, factor, first):
    half = normed.shape[1] // 2
    left, right = normed[:, :half], normed[:, half:]

    def product(columns):
        value = lax.dot_general(
            columns, masked, (((0,), (0,)), ((), ())), preferred_element_type=F32
        )
        return (value * factor).astype(BF16)

    came = over_rep(product(jnp.where(first, right, left)), X_SWAP)
    both = add(product(jnp.where(first, left, right)), came)
    return lax.psum_scatter(
        both, "rep", scatter_dimension=0, tiled=True, axis_index_groups=Y_RINGS
    )


def sum_over_col(partial, z):
    def residue(step):
        return lax.rem(z + step + NZ, 4)

    def near(pieces):
        return (
            near_two(pieces[0]),
            over_col(pieces[1], 1),
            over_col(pieces[2], -1),
        )

    arrived = near((partial(2), partial(1), partial(-1)))
    mine = add(partial(0), *arrived)
    below = over_col(mine, 4)
    above = over_col(mine, -4)
    q = z // 4
    last = jnp.where(q == 0, below, jnp.where(q == 1, above, mine))
    one = jnp.where(q == 0, mine, below)
    two = jnp.where(q == 1, mine, above)
    total = add(one, two, last)
    arrived = near((total, total, total))
    result = jnp.zeros((4,) + total.shape, total.dtype)
    for step, value in ((0, total), (2, arrived[0]), (-1, arrived[1]), (1, arrived[2])):
        result = lax.dynamic_update_slice(result, value[None], (residue(step), 0, 0))
    return result.reshape(-1, total.shape[1])


def body(normed, up_weight, cotangent, lengths):
    row_count, width = normed.shape
    pair_count = lengths.shape[0]
    pair_len = row_count // pair_count
    keep_rows, unit_count = up_weight.shape[1:]
    first = lax.axis_index("rep") < NY
    z = lax.axis_index("col")

    weight = gather_weight(up_weight)

    positions = lax.broadcasted_iota(jnp.int32, (pair_count, pair_len), 1)
    valid_rows = (positions < lengths[:, None]).reshape(row_count, 1)
    masked = jnp.where(valid_rows, cotangent, jnp.zeros_like(cotangent))

    factor = 1.0 / math.sqrt(row_count * lax.axis_size("rep"))
    weight_grad = scatter_wgrad(normed, masked, factor, first)
    weight_grad = weight_grad.reshape(1, keep_rows, unit_count)

    quarters = masked.reshape(4, row_count // 4, unit_count)

    turned = lax.optimization_barrier(
        tuple(
            lax.dynamic_index_in_dim(quarters, lax.rem(z + s, 4), 0, keepdims=False)
            for s in range(4)
        )
    )

    def partial_grad(step):
        value = lax.dot_general(
            turned[step % 4],
            weight,
            (((1,), (1,)), ((), ())),
            preferred_element_type=F32,
        )
        return value.astype(BF16)

    normed_grad = sum_over_col(partial_grad, z)

    up_partial = jnp.dot(normed, weight, preferred_element_type=F32)
    up_out = lax.psum_scatter(
        up_partial.astype(BF16), "row", scatter_dimension=0, tiled=True
    )
    return (up_out, normed_grad, weight_grad)


def solution(mesh):
    placed = (P("rep", "row"), P("row", "rep", "col"), P("rep", "col"), P("rep"))
    return jax.shard_map(
        body,
        mesh=mesh,
        in_specs=placed,
        out_specs=(P(("rep", "row"), "col"), P("rep", "row"), P("row", "rep", "col")),
        check_vma=False,
    )
```

```python
import math

import jax
import jax.numpy as jnp
from jax import lax
from jax.sharding import PartitionSpec as P

NY = 8
NZ = 12
F32 = jnp.float32
BF16 = jnp.bfloat16

Y_RINGS = [[h * NY + y for y in range(NY)] for h in range(2)]
X_PAIRS = [[y, y + NY] for y in range(NY)]
X_SWAP = [(i, (i + NY) % (2 * NY)) for i in range(2 * NY)]


def z_shift(step):
    return [(z, (z + step) % NZ) for z in range(NZ)]


def over_rep(value, pairs):
    return lax.ppermute(value, "rep", pairs)


def over_col(value, step):
    return lax.ppermute(value, "col", z_shift(step))


def near_two(value):
    pairs = []
    for row in range(4):
        step = 2 - 4 * (row % 2)
        pairs += [(row * NZ + z, row * NZ + (z + step) % NZ) for z in range(NZ)]
    return lax.ppermute(value, ("row", "col"), pairs)


def add(*terms):
    total = terms[0].astype(F32)
    for term in terms[1:]:
        total = total + term.astype(F32)
    return total.astype(BF16)


def gather_weight(w0):
    pair = lax.all_gather(w0, "rep", axis=0, tiled=True, axis_index_groups=X_PAIRS)
    whole = lax.all_gather(pair, "rep", axis=1, tiled=True, axis_index_groups=Y_RINGS)
    return whole.reshape(-1, w0.shape[2])


def scatter_wgrad(normed, masked, factor, first):
    half = normed.shape[1] // 2
    left, right = normed[:, :half], normed[:, half:]

    def product(columns):
        value = lax.dot_general(
            columns, masked, (((0,), (0,)), ((), ())), preferred_element_type=F32
        )
        return (value * factor).astype(BF16)

    came = over_rep(product(jnp.where(first, right, left)), X_SWAP)
    both = add(product(jnp.where(first, left, right)), came)
    return lax.psum_scatter(
        both, "rep", scatter_dimension=0, tiled=True, axis_index_groups=Y_RINGS
    )


def sum_over_col(partial, z):
    def residue(step):
        return lax.rem(z + step + NZ, 4)

    def near(pieces):
        return (
            near_two(pieces[0]),
            over_col(pieces[1], 1),
            over_col(pieces[2], -1),
        )

    arrived = near((partial(2), partial(1), partial(-1)))
    mine = add(partial(0), *arrived)
    below = over_col(mine, 4)
    above = over_col(mine, -4)
    q = z // 4
    last = jnp.where(q == 0, below, jnp.where(q == 1, above, mine))
    one = jnp.where(q == 0, mine, below)
    two = jnp.where(q == 1, mine, above)
    total = add(one, two, last)
    arrived = near((total, total, total))
    result = jnp.zeros((4,) + total.shape, total.dtype)
    for step, value in ((0, total), (2, arrived[0]), (-1, arrived[1]), (1, arrived[2])):
        result = lax.dynamic_update_slice(result, value[None], (residue(step), 0, 0))
    return result.reshape(-1, total.shape[1])


def body(normed, up_weight, cotangent, lengths):
    row_count, width = normed.shape
    pair_count = lengths.shape[0]
    pair_len = row_count // pair_count
    keep_rows, unit_count = up_weight.shape[1:]
    first = lax.axis_index("rep") < NY
    z = lax.axis_index("col")

    weight = gather_weight(up_weight)

    positions = lax.broadcasted_iota(jnp.int32, (pair_count, pair_len), 1)
    valid_rows = (positions < lengths[:, None]).reshape(row_count, 1)
    masked = jnp.where(valid_rows, cotangent, jnp.zeros_like(cotangent))

    factor = 1.0 / math.sqrt(row_count * lax.axis_size("rep"))
    weight_grad = scatter_wgrad(normed, masked, factor, first)
    weight_grad = weight_grad.reshape(1, keep_rows, unit_count)

    quarters = masked.reshape(4, row_count // 4, unit_count)

    turned = lax.optimization_barrier(
        tuple(
            lax.dynamic_index_in_dim(quarters, lax.rem(z + s, 4), 0, keepdims=False)
            for s in range(4)
        )
    )

    def grad_of(rows):
        def partial(step):
            value = lax.dot_general(
                turned[step % 4],
                rows,
                (((1,), (1,)), ((), ())),
                preferred_element_type=F32,
            )
            return value.astype(BF16)

        return sum_over_col(partial, z)

    half = width // 2
    normed_grad = jnp.concatenate(
        [grad_of(weight[:half]), grad_of(weight[half:])], axis=1
    )

    up_partial = jnp.dot(normed, weight, preferred_element_type=F32)
    up_out = lax.psum_scatter(
        up_partial.astype(BF16), "row", scatter_dimension=0, tiled=True
    )
    return (up_out, normed_grad, weight_grad)


def solution(mesh):
    placed = (P("rep", "row"), P("row", "rep", "col"), P("rep", "col"), P("rep"))
    return jax.shard_map(
        body,
        mesh=mesh,
        in_specs=placed,
        out_specs=(P(("rep", "row"), "col"), P("rep", "row"), P("row", "rep", "col")),
        check_vma=False,
    )
```

```python
import math

import jax
import jax.numpy as jnp
from jax import lax
from jax.sharding import PartitionSpec as P

NY = 8
NZ = 12
F32 = jnp.float32
BF16 = jnp.bfloat16

Y_RINGS = [[h * NY + y for y in range(NY)] for h in range(2)]
X_PAIRS = [[y, y + NY] for y in range(NY)]
X_SWAP = [(i, (i + NY) % (2 * NY)) for i in range(2 * NY)]


def over_rep(value, pairs):
    return lax.ppermute(value, "rep", pairs)


def over_col(value, step):
    pairs = []
    for row in range(4):
        signed = step - 2 * step * (row % 2)
        pairs += [(row * NZ + z, row * NZ + (z + signed) % NZ) for z in range(NZ)]
    return lax.ppermute(value, ("row", "col"), pairs)


def add(*terms):
    total = terms[0].astype(F32)
    for term in terms[1:]:
        total = total + term.astype(F32)
    return total.astype(BF16)


def gather_weight(w0):
    pair = lax.all_gather(w0, "rep", axis=0, tiled=True, axis_index_groups=X_PAIRS)
    whole = lax.all_gather(pair, "rep", axis=1, tiled=True, axis_index_groups=Y_RINGS)
    return whole.reshape(-1, w0.shape[2])


def scatter_wgrad(normed, masked, factor, first):
    half = normed.shape[1] // 2
    left, right = normed[:, :half], normed[:, half:]

    def product(columns):
        value = lax.dot_general(
            columns, masked, (((0,), (0,)), ((), ())), preferred_element_type=F32
        )
        return (value * factor).astype(BF16)

    came = over_rep(product(jnp.where(first, right, left)), X_SWAP)
    both = add(product(jnp.where(first, left, right)), came)
    return lax.psum_scatter(
        both, "rep", scatter_dimension=0, tiled=True, axis_index_groups=Y_RINGS
    )


def sum_over_col(turned, weight, z, up):
    def partial(tokens):
        value = lax.dot_general(
            tokens, weight, (((1,), (1,)), ((), ())), preferred_element_type=F32
        )
        return value.astype(BF16)

    two_away = partial(turned[2])
    ahead, behind, _ = lax.optimization_barrier((turned[1], turned[3], two_away))
    arrived = (
        over_col(two_away, 2),
        over_col(partial(ahead), 1),
        over_col(partial(behind), -1),
    )
    mine = add(partial(turned[0]), *arrived)
    from_behind = over_col(mine, 4)
    from_ahead = over_col(mine, -4)
    below = jnp.where(up == 1, from_behind, from_ahead)
    above = jnp.where(up == 1, from_ahead, from_behind)
    q = z // 4
    last = jnp.where(q == 0, below, jnp.where(q == 1, above, mine))
    one = jnp.where(q == 0, mine, below)
    two = jnp.where(q == 1, mine, above)
    total = add(one, two, last)
    arrived = (over_col(total, 2), over_col(total, 1), over_col(total, -1))
    result = jnp.zeros((4,) + total.shape, total.dtype)
    for step, value in ((0, total), (2, arrived[0]), (-1, arrived[1]), (1, arrived[2])):
        place = lax.rem(z + step * up + NZ, 4)
        result = lax.dynamic_update_slice(result, value[None], (place, 0, 0))
    return result.reshape(-1, total.shape[1])


def body(normed, up_weight, cotangent, lengths):
    row_count, width = normed.shape
    pair_count = lengths.shape[0]
    pair_len = row_count // pair_count
    keep_rows, unit_count = up_weight.shape[1:]
    first = lax.axis_index("rep") < NY
    z = lax.axis_index("col")

    weight = gather_weight(up_weight)

    positions = lax.broadcasted_iota(jnp.int32, (pair_count, pair_len), 1)
    valid_rows = (positions < lengths[:, None]).reshape(row_count, 1)
    masked = jnp.where(valid_rows, cotangent, jnp.zeros_like(cotangent))

    factor = 1.0 / math.sqrt(row_count * lax.axis_size("rep"))
    weight_grad = scatter_wgrad(normed, masked, factor, first)
    weight_grad = weight_grad.reshape(1, keep_rows, unit_count)

    quarters = masked.reshape(4, row_count // 4, unit_count)

    up = 1 - 2 * lax.rem(lax.axis_index("row"), 2)
    turned = lax.optimization_barrier(
        tuple(
            lax.dynamic_index_in_dim(quarters, lax.rem(z + s * up + NZ, 4), 0, keepdims=False)
            for s in range(4)
        )
    )
    normed_grad = sum_over_col(turned, weight, z, up)

    up_partial = jnp.dot(normed, weight, preferred_element_type=F32)
    up_out = lax.psum_scatter(
        up_partial.astype(BF16), "row", scatter_dimension=0, tiled=True
    )
    return (up_out, normed_grad, weight_grad)


def solution(mesh):
    placed = (P("rep", "row"), P("row", "rep", "col"), P("rep", "col"), P("rep"))
    return jax.shard_map(
        body,
        mesh=mesh,
        in_specs=placed,
        out_specs=(P(("rep", "row"), "col"), P("rep", "row"), P("row", "rep", "col")),
        check_vma=False,
    )
```

```python
import math

import jax
import jax.numpy as jnp
from jax import lax
from jax.sharding import PartitionSpec as P

NY = 8
NZ = 12
F32 = jnp.float32
BF16 = jnp.bfloat16

Y_RINGS = [[h * NY + y for y in range(NY)] for h in range(2)]
X_SWAP = [(i, (i + NY) % (2 * NY)) for i in range(2 * NY)]


def y_shift(step):
    return [(h * NY + y, h * NY + (y + step) % NY) for h in range(2) for y in range(NY)]


def over_rep(value, pairs):
    return lax.ppermute(value, "rep", pairs)


def over_col(value, step):
    pairs = []
    for row in range(4):
        signed = step - 2 * step * (row % 2)
        pairs += [(row * NZ + z, row * NZ + (z + signed) % NZ) for z in range(NZ)]
    return lax.ppermute(value, ("row", "col"), pairs)


def add(*terms):
    total = terms[0].astype(F32)
    for term in terms[1:]:
        total = total + term.astype(F32)
    return total.astype(BF16)


def gather_weight(w0, y):
    own = lax.all_gather(w0, "rep", axis=0, tiled=True, axis_index_groups=Y_RINGS)
    there = over_rep(w0, X_SWAP)
    from_m3 = over_rep(there, y_shift(3))
    from_p3 = over_rep(there, y_shift(-3))
    from_m1 = over_rep(jnp.concatenate([there, from_p3, from_m3]), y_shift(1))
    from_p1 = over_rep(jnp.concatenate([there, from_m3]), y_shift(-1))
    whole = jnp.zeros((2 * NY,) + w0.shape[1:], w0.dtype)
    for source, steps in (
        (there, (0,)),
        (from_m3, (-3,)),
        (from_p3, (3,)),
        (from_m1, (-1, 2, 4)),
        (from_p1, (1, -2)),
    ):
        for slot, step in enumerate(steps):
            place = NY + lax.rem(y + step + NY, NY)
            whole = lax.dynamic_update_slice(
                whole, source[slot : slot + 1], (place, 0, 0)
            )
    whole = lax.dynamic_update_slice(whole, own, (0, 0, 0))
    return whole.reshape(-1, w0.shape[2])


def scatter_wgrad(normed, masked, factor, x_hi, keep_rows):
    half = normed.shape[1] // 2

    def product(columns):
        value = lax.dot_general(
            columns, masked, (((0,), (0,)), ((), ())), preferred_element_type=F32
        )
        return (value * factor).astype(BF16).reshape(NY, keep_rows, -1)

    value = jnp.stack([product(normed[:, :half]), product(normed[:, half:])], axis=1)
    pair = lax.psum_scatter(
        value.reshape(2 * NY, keep_rows, -1),
        "rep",
        scatter_dimension=0,
        tiled=True,
        axis_index_groups=Y_RINGS,
    )
    kept = lax.dynamic_index_in_dim(pair, x_hi, 0)
    sent = lax.dynamic_index_in_dim(pair, 1 - x_hi, 0)
    return kept, over_rep(sent, X_SWAP)


def sum_over_col(turned, weight, z, up, in_order, ready):
    def partial(tokens):
        value = lax.dot_general(
            tokens, weight, (((1,), (1,)), ((), ())), preferred_element_type=F32
        )
        return value.astype(BF16)

    two_away = partial(turned[2])
    ahead, behind, _ = lax.optimization_barrier((turned[1], turned[3], two_away))
    arrived = (
        over_col(two_away, 2),
        over_col(partial(ahead), 1),
        over_col(partial(behind), -1),
    )
    mine = add(partial(turned[0]), *arrived)
    from_behind = over_col(mine, 4)
    from_ahead = over_col(mine, -4)
    below = jnp.where(up == 1, from_behind, from_ahead)
    above = jnp.where(up == 1, from_ahead, from_behind)
    q = z // 4
    last = jnp.where(q == 0, below, jnp.where(q == 1, above, mine))
    one = jnp.where(q == 0, mine, below)
    two = jnp.where(q == 1, mine, above)
    total = in_order(add(one, two, last))
    total, _ = lax.optimization_barrier((total, ready))
    arrived = (over_col(total, 2), over_col(total, 1), over_col(total, -1))
    result = jnp.zeros((4,) + total.shape, total.dtype)
    for step, value in ((0, total), (2, arrived[0]), (-1, arrived[1]), (1, arrived[2])):
        place = lax.rem(z + step * up + NZ, 4)
        result = lax.dynamic_update_slice(result, value[None], (place, 0, 0))
    return result.reshape(-1, total.shape[1])


def body(normed, up_weight, cotangent, lengths):
    row_count, width = normed.shape
    pair_count = lengths.shape[0]
    pair_len = row_count // pair_count
    keep_rows, unit_count = up_weight.shape[1:]
    rep = lax.axis_index("rep")
    first = rep < NY
    z = lax.axis_index("col")

    def swap_halves(columns):
        left, right = columns[:, : width // 2], columns[:, width // 2 :]
        return jnp.concatenate(
            [jnp.where(first, left, right), jnp.where(first, right, left)], axis=1
        )

    weight = gather_weight(up_weight, lax.rem(rep, NY))

    positions = lax.broadcasted_iota(jnp.int32, (pair_count, pair_len), 1)
    valid_rows = (positions < lengths[:, None]).reshape(row_count, 1)
    masked = jnp.where(valid_rows, cotangent, jnp.zeros_like(cotangent))

    factor = 1.0 / math.sqrt(row_count * lax.axis_size("rep"))
    kept, came = scatter_wgrad(normed, masked, factor, rep // NY, keep_rows)
    weight_grad = add(kept, came)

    quarters = masked.reshape(4, row_count // 4, unit_count)

    up = 1 - 2 * lax.rem(lax.axis_index("row"), 2)
    turned = lax.optimization_barrier(
        tuple(
            lax.dynamic_index_in_dim(quarters, lax.rem(z + s * up + NZ, 4), 0, keepdims=False)
            for s in range(4)
        )
    )
    normed_grad = sum_over_col(turned, weight, z, up, swap_halves, came)

    up_partial = jnp.dot(swap_halves(normed), weight, preferred_element_type=F32)
    up_out = lax.psum_scatter(
        up_partial.astype(BF16), "row", scatter_dimension=0, tiled=True
    )
    return (up_out, normed_grad, weight_grad)


def solution(mesh):
    placed = (P("rep", "row"), P("row", "rep", "col"), P("rep", "col"), P("rep"))
    return jax.shard_map(
        body,
        mesh=mesh,
        in_specs=placed,
        out_specs=(P(("rep", "row"), "col"), P("rep", "row"), P("row", "rep", "col")),
        check_vma=False,
    )
```

```python
import math

import jax
import jax.numpy as jnp
from jax import lax
from jax.sharding import PartitionSpec as P

NY = 8
NZ = 12
F32 = jnp.float32
BF16 = jnp.bfloat16

Y_RINGS = [[h * NY + y for y in range(NY)] for h in range(2)]
X_PAIRS = [[y, y + NY] for y in range(NY)]
X_SWAP = [(i, (i + NY) % (2 * NY)) for i in range(2 * NY)]


def over_rep(value, pairs):
    return lax.ppermute(value, "rep", pairs)


def over_col(value, step):
    pairs = []
    for row in range(4):
        signed = step - 2 * step * (row % 2)
        pairs += [(row * NZ + z, row * NZ + (z + signed) % NZ) for z in range(NZ)]
    return lax.ppermute(value, ("row", "col"), pairs)


def add(*terms):
    total = terms[0].astype(F32)
    for term in terms[1:]:
        total = total + term.astype(F32)
    return total.astype(BF16)


def gather_weight(w0):
    pair = lax.all_gather(w0, "rep", axis=0, tiled=True, axis_index_groups=X_PAIRS)
    whole = lax.all_gather(pair, "rep", axis=1, tiled=True, axis_index_groups=Y_RINGS)
    return whole.reshape(-1, w0.shape[2])


def scatter_wgrad(normed, masked, factor, first):
    half = normed.shape[1] // 2
    left, right = normed[:, :half], normed[:, half:]

    def product(columns):
        value = lax.dot_general(
            columns, masked, (((0,), (0,)), ((), ())), preferred_element_type=F32
        )
        return (value * factor).astype(BF16)

    came = over_rep(product(jnp.where(first, right, left)), X_SWAP)
    both = add(product(jnp.where(first, left, right)), came)
    return lax.psum_scatter(
        both, "rep", scatter_dimension=0, tiled=True, axis_index_groups=Y_RINGS
    )


def sum_over_col(turned, weight, z, up):
    products = lax.dot_general(
        turned, weight, (((1,), (1,)), ((), ())), preferred_element_type=F32
    )
    two_away, ahead, behind, kept = jnp.split(products.astype(BF16), 4)
    arrived = (over_col(two_away, 2), over_col(ahead, 1), over_col(behind, -1))
    mine = add(kept, *arrived)
    from_behind = over_col(mine, 4)
    from_ahead = over_col(mine, -4)
    below = jnp.where(up == 1, from_behind, from_ahead)
    above = jnp.where(up == 1, from_ahead, from_behind)
    q = z // 4
    last = jnp.where(q == 0, below, jnp.where(q == 1, above, mine))
    one = jnp.where(q == 0, mine, below)
    two = jnp.where(q == 1, mine, above)
    total = add(one, two, last)
    arrived = (over_col(total, 2), over_col(total, 1), over_col(total, -1))
    result = jnp.zeros((4,) + total.shape, total.dtype)
    for step, value in ((0, total), (2, arrived[0]), (-1, arrived[1]), (1, arrived[2])):
        place = lax.rem(z + step * up + NZ, 4)
        result = lax.dynamic_update_slice(result, value[None], (place, 0, 0))
    return result.reshape(-1, total.shape[1])


def body(normed, up_weight, cotangent, lengths):
    row_count, width = normed.shape
    pair_count = lengths.shape[0]
    pair_len = row_count // pair_count
    keep_rows, unit_count = up_weight.shape[1:]
    first = lax.axis_index("rep") < NY
    z = lax.axis_index("col")

    weight = gather_weight(up_weight)

    positions = lax.broadcasted_iota(jnp.int32, (pair_count, pair_len), 1)
    valid_rows = (positions < lengths[:, None]).reshape(row_count, 1)
    masked = jnp.where(valid_rows, cotangent, jnp.zeros_like(cotangent))

    factor = 1.0 / math.sqrt(row_count * lax.axis_size("rep"))
    weight_grad = scatter_wgrad(normed, masked, factor, first)
    weight_grad = weight_grad.reshape(1, keep_rows, unit_count)

    quarters = masked.reshape(4, row_count // 4, unit_count)

    up = 1 - 2 * lax.rem(lax.axis_index("row"), 2)
    turned = lax.optimization_barrier(
        jnp.concatenate(
            [
                lax.dynamic_index_in_dim(
                    quarters, lax.rem(z + s * up + NZ, 4), 0, keepdims=False
                )
                for s in (2, 1, -1, 0)
            ]
        )
    )
    normed_grad = sum_over_col(turned, weight, z, up)

    up_partial = jnp.dot(normed, weight, preferred_element_type=F32)
    up_out = lax.psum_scatter(
        up_partial.astype(BF16), "row", scatter_dimension=0, tiled=True
    )
    return (up_out, normed_grad, weight_grad)


def solution(mesh):
    placed = (P("rep", "row"), P("row", "rep", "col"), P("rep", "col"), P("rep"))
    return jax.shard_map(
        body,
        mesh=mesh,
        in_specs=placed,
        out_specs=(P(("rep", "row"), "col"), P("rep", "row"), P("row", "rep", "col")),
        check_vma=False,
    )
```

```python
import math

import jax
import jax.numpy as jnp
from jax import lax
from jax.sharding import PartitionSpec as P

NY = 8
NZ = 12
F32 = jnp.float32
BF16 = jnp.bfloat16

Y_RINGS = [[h * NY + y for y in range(NY)] for h in range(2)]
X_PAIRS = [[y, y + NY] for y in range(NY)]
X_SWAP = [(i, (i + NY) % (2 * NY)) for i in range(2 * NY)]


def over_rep(value, pairs):
    return lax.ppermute(value, "rep", pairs)


def over_col(value, step):
    pairs = []
    for row in range(4):
        signed = step - 2 * step * (row % 2)
        pairs += [(row * NZ + z, row * NZ + (z + signed) % NZ) for z in range(NZ)]
    return lax.ppermute(value, ("row", "col"), pairs)


def add(*terms):
    total = terms[0].astype(F32)
    for term in terms[1:]:
        total = total + term.astype(F32)
    return total.astype(BF16)


def gather_weight(w0):
    pair = lax.all_gather(w0, "rep", axis=0, tiled=True, axis_index_groups=X_PAIRS)
    whole = lax.all_gather(pair, "rep", axis=1, tiled=True, axis_index_groups=Y_RINGS)
    return whole.reshape(-1, w0.shape[2])


def scatter_wgrad(normed, masked, factor, first):
    half = normed.shape[1] // 2
    left, right = normed[:, :half], normed[:, half:]

    def product(columns):
        value = lax.dot_general(
            columns, masked, (((0,), (0,)), ((), ())), preferred_element_type=F32
        )
        return (value * factor).astype(BF16)

    came = over_rep(product(jnp.where(first, right, left)), X_SWAP)
    both = add(product(jnp.where(first, left, right)), came)
    return lax.psum_scatter(
        both, "rep", scatter_dimension=0, tiled=True, axis_index_groups=Y_RINGS
    )


def sum_over_col(turned, weight, z, up):
    products = lax.dot_general(
        turned, weight, (((1,), (1,)), ((), ())), preferred_element_type=F32
    )
    two_away, ahead, behind, kept = jnp.split(products.astype(BF16), 4)
    arrived = (over_col(two_away, 2), over_col(ahead, 1), over_col(behind, -1))
    mine = add(kept, *arrived)
    q = z // 4
    half = mine.shape[1] // 2
    parts = (mine[:, :half], mine[:, half:])
    moved = [(over_col(part, 4), over_col(part, -4)) for part in parts]
    results = []
    for part, (from_behind, from_ahead) in zip(parts, moved):
        below = jnp.where(up == 1, from_behind, from_ahead)
        above = jnp.where(up == 1, from_ahead, from_behind)
        last = jnp.where(q == 0, below, jnp.where(q == 1, above, part))
        one = jnp.where(q == 0, part, below)
        two = jnp.where(q == 1, part, above)
        total = add(one, two, last)
        result = jnp.zeros((4,) + total.shape, total.dtype)
        for step, value in (
            (0, total),
            (2, over_col(total, 2)),
            (-1, over_col(total, 1)),
            (1, over_col(total, -1)),
        ):
            place = lax.rem(z + step * up + NZ, 4)
            result = lax.dynamic_update_slice(result, value[None], (place, 0, 0))
        results.append(result.reshape(-1, half))
    return jnp.concatenate(results, axis=1)


def body(normed, up_weight, cotangent, lengths):
    row_count, width = normed.shape
    pair_count = lengths.shape[0]
    pair_len = row_count // pair_count
    keep_rows, unit_count = up_weight.shape[1:]
    first = lax.axis_index("rep") < NY
    z = lax.axis_index("col")

    weight = gather_weight(up_weight)

    positions = lax.broadcasted_iota(jnp.int32, (pair_count, pair_len), 1)
    valid_rows = (positions < lengths[:, None]).reshape(row_count, 1)
    masked = jnp.where(valid_rows, cotangent, jnp.zeros_like(cotangent))

    factor = 1.0 / math.sqrt(row_count * lax.axis_size("rep"))
    weight_grad = scatter_wgrad(normed, masked, factor, first)
    weight_grad = weight_grad.reshape(1, keep_rows, unit_count)

    quarters = masked.reshape(4, row_count // 4, unit_count)

    up = 1 - 2 * lax.rem(lax.axis_index("row"), 2)
    turned = lax.optimization_barrier(
        jnp.concatenate(
            [
                lax.dynamic_index_in_dim(
                    quarters, lax.rem(z + s * up + NZ, 4), 0, keepdims=False
                )
                for s in (2, 1, -1, 0)
            ]
        )
    )
    normed_grad = sum_over_col(turned, weight, z, up)

    up_partial = jnp.dot(normed, weight, preferred_element_type=F32)
    up_out = lax.psum_scatter(
        up_partial.astype(BF16), "row", scatter_dimension=0, tiled=True
    )
    return (up_out, normed_grad, weight_grad)


def solution(mesh):
    placed = (P("rep", "row"), P("row", "rep", "col"), P("rep", "col"), P("rep"))
    return jax.shard_map(
        body,
        mesh=mesh,
        in_specs=placed,
        out_specs=(P(("rep", "row"), "col"), P("rep", "row"), P("row", "rep", "col")),
        check_vma=False,
    )
```

```python
import math

import jax
import jax.numpy as jnp
from jax import lax
from jax.sharding import PartitionSpec as P

NY = 8
NZ = 12
F32 = jnp.float32
BF16 = jnp.bfloat16

Y_RINGS = [[h * NY + y for y in range(NY)] for h in range(2)]
X_PAIRS = [[y, y + NY] for y in range(NY)]
X_SWAP = [(i, (i + NY) % (2 * NY)) for i in range(2 * NY)]


def over_rep(value, pairs):
    return lax.ppermute(value, "rep", pairs)


def over_col(value, step):
    pairs = []
    for row in range(4):
        signed = step - 2 * step * (row % 2)
        pairs += [(row * NZ + z, row * NZ + (z + signed) % NZ) for z in range(NZ)]
    return lax.ppermute(value, ("row", "col"), pairs)


def add(*terms):
    total = terms[0].astype(F32)
    for term in terms[1:]:
        total = total + term.astype(F32)
    return total.astype(BF16)


def gather_weight(w0):
    pair = lax.all_gather(w0, "rep", axis=0, tiled=True, axis_index_groups=X_PAIRS)
    whole = lax.all_gather(pair, "rep", axis=1, tiled=True, axis_index_groups=Y_RINGS)
    return whole.reshape(-1, w0.shape[2])


def scatter_wgrad(normed, masked, factor, first):
    half = normed.shape[1] // 2
    left, right = normed[:, :half], normed[:, half:]

    def product(columns):
        value = lax.dot_general(
            columns, masked, (((0,), (0,)), ((), ())), preferred_element_type=F32
        )
        return (value * factor).astype(BF16)

    came = over_rep(product(jnp.where(first, right, left)), X_SWAP)
    both = add(product(jnp.where(first, left, right)), came)
    return lax.psum_scatter(
        both, "rep", scatter_dimension=0, tiled=True, axis_index_groups=Y_RINGS
    )


def sum_over_col(turned, weight, z, up):
    def partial(tokens):
        value = lax.dot_general(
            tokens, weight, (((1,), (1,)), ((), ())), preferred_element_type=F32
        )
        return value.astype(BF16)

    two_away = partial(turned[2])
    ahead, behind, _ = lax.optimization_barrier((turned[1], turned[3], two_away))
    from_back = over_col(partial(behind), -1)
    from_front = over_col(partial(ahead), 1)
    arrived = (over_col(two_away, 2), from_front, from_back)
    mine = add(partial(turned[0]), *arrived)
    from_behind = over_col(mine, 4)
    from_ahead = over_col(mine, -4)
    below = jnp.where(up == 1, from_behind, from_ahead)
    above = jnp.where(up == 1, from_ahead, from_behind)
    q = z // 4
    last = jnp.where(q == 0, below, jnp.where(q == 1, above, mine))
    one = jnp.where(q == 0, mine, below)
    two = jnp.where(q == 1, mine, above)
    total = add(one, two, last)
    arrived = (over_col(total, 2), over_col(total, 1), over_col(total, -1))
    result = jnp.zeros((4,) + total.shape, total.dtype)
    for step, value in ((0, total), (2, arrived[0]), (-1, arrived[1]), (1, arrived[2])):
        place = lax.rem(z + step * up + NZ, 4)
        result = lax.dynamic_update_slice(result, value[None], (place, 0, 0))
    return result.reshape(-1, total.shape[1])


def body(normed, up_weight, cotangent, lengths):
    row_count, width = normed.shape
    pair_count = lengths.shape[0]
    pair_len = row_count // pair_count
    keep_rows, unit_count = up_weight.shape[1:]
    first = lax.axis_index("rep") < NY
    z = lax.axis_index("col")

    weight = gather_weight(up_weight)

    positions = lax.broadcasted_iota(jnp.int32, (pair_count, pair_len), 1)
    valid_rows = (positions < lengths[:, None]).reshape(row_count, 1)
    masked = jnp.where(valid_rows, cotangent, jnp.zeros_like(cotangent))

    factor = 1.0 / math.sqrt(row_count * lax.axis_size("rep"))
    weight_grad = scatter_wgrad(normed, masked, factor, first)
    weight_grad = weight_grad.reshape(1, keep_rows, unit_count)

    quarters = masked.reshape(4, row_count // 4, unit_count)

    up = 1 - 2 * lax.rem(lax.axis_index("row"), 2)
    turned = lax.optimization_barrier(
        tuple(
            lax.dynamic_index_in_dim(quarters, lax.rem(z + s * up + NZ, 4), 0, keepdims=False)
            for s in range(4)
        )
    )
    normed_grad = sum_over_col(turned, weight, z, up)

    up_partial = jnp.dot(normed, weight, preferred_element_type=F32)
    up_out = lax.psum_scatter(
        up_partial.astype(BF16), "row", scatter_dimension=0, tiled=True
    )
    return (up_out, normed_grad, weight_grad)


def solution(mesh):
    placed = (P("rep", "row"), P("row", "rep", "col"), P("rep", "col"), P("rep"))
    return jax.shard_map(
        body,
        mesh=mesh,
        in_specs=placed,
        out_specs=(P(("rep", "row"), "col"), P("rep", "row"), P("row", "rep", "col")),
        check_vma=False,
    )
```
